32 devices in a mesh: layer: 2 (over y), facet: 16 (over z, x, core).
Axes of the slice: x: 2, y: 2, z: 4, core: 2. Of those that a mesh axis runs over, the one named last changes fastest.
Arguments:
- slabs: bfloat16 [2, 2, 64, 49152], P('layer', None, None, 'facet'), may hold values from -6 to 6
- window: float32 [49152], P('facet'), may hold values from 0.5 to 1.5
- density: int32 [2, 64, 8192], P('layer', None, 'facet'), may hold values from 0 to 7
- offsets: int32 [16], replicated, may hold values from 0 to 49151
Outputs:
- image_out: float32 [2, 64, 49152], P(None, 'layer', 'facet')
The draws below stay inside these ranges and needn't reach their ends.
All inputs are finite; a program needn't handle non-finite values.
Results may differ from the reference program's by a relative error of at most 0.0052.
Values may be sent and summed in bfloat16 or wider, within the bound.
A program may use at most 64 MiB of HBM per device.

```python
import math
import jax
import jax.numpy as jnp
from jax import lax

FACET = 3072
CONTRIB = 128
SUB = 512
COLS = 64
LAYERS = 2
FACETS = 16
IMAGE = 49152


def touch_ends(drawn, rng, smallest, largest):
    longest = drawn.shape.index(max(drawn.shape))
    spots = []
    for shift in (0, 1):
        where = [jax.random.randint(jax.random.fold_in(rng, axis), (), 0, length) for axis, length in enumerate(drawn.shape)]
        where[longest] = (where[longest] + shift) % drawn.shape[longest]
        spots.append(tuple(where))
    return drawn.at[spots[0]].set(smallest).at[spots[1]].set(largest)


def levels(stream_key, extent, shards, least, top_value):
    def one(dim, blocks):
        steps = jax.random.uniform(jax.random.fold_in(jax.random.fold_in(stream_key, 6), dim), (blocks,), jnp.float32, least / len(shards), top_value / len(shards))
        return jnp.repeat(jnp.exp(steps), extent[dim] // blocks).reshape((-1,) + (1,) * (len(extent) - dim - 1))

    gain = one(*shards[0])
    for cut in shards[1:]:
        gain = gain * one(*cut)
    return gain


def gaussian(own_key, shape, spread, most, shards=(), held_as=jnp.bfloat16):
    gain = levels(own_key, shape, shards, -0.22, 0.18) if shards else 1.0
    result = jax.random.normal(own_key, shape, jnp.float32) * spread * gain
    return jnp.minimum(jnp.maximum(result, -most), most).astype(held_as)


def setup_inputs(seed: int = 0) -> dict:
    streams_of = jax.random.split(jax.random.key(seed), 5)
    return {
        "slabs": gaussian(streams_of[0], (LAYERS, 2, COLS, IMAGE), 1.0, 6.0, ((0, 2), (3, 16))),
        "window": jnp.clip(0.5 + 1.0 * jax.random.uniform(streams_of[1], (IMAGE,), jnp.float32) ** levels(streams_of[1], (IMAGE,), ((0, 16),), -0.2, 0.2), 0.5, 1.5),
        "density": touch_ends(jax.random.randint(streams_of[2], (LAYERS, COLS, FACETS * SUB), 0, 8), jax.random.fold_in(streams_of[2], 1), 0, 7).astype(jnp.int32),
        "offsets": touch_ends(jax.random.randint(streams_of[3], (FACETS,), 0, IMAGE), jax.random.fold_in(streams_of[3], 1), 0, IMAGE - 1).astype(jnp.int32),
    }


two_pi = 2.0 * math.pi


def mulmod(left_term, right_term, modulus):
    upper_part = right_term // 256
    lower_part = right_term % 256
    return jnp.mod(jnp.mod(left_term * upper_part, modulus) * 256 + left_term * lower_part, modulus)


def encode_table(offset_block, x_start, facet_width, contrib_len, sample_step, image_width):
    frequencies = jnp.mod(offset_block[:, None] + sample_step * jnp.arange(contrib_len, dtype=jnp.int32)[None, :], image_width)
    places = x_start + jnp.arange(facet_width, dtype=jnp.int32)
    phase_turns = mulmod(frequencies[:, :, None], places[None, None, :], image_width)
    phase_angle = phase_turns.astype(jnp.float32) * (-two_pi / image_width)
    return jnp.stack([jnp.cos(phase_angle), jnp.sin(phase_angle)], 1).astype(jnp.bfloat16)


def embed_table(facet_count, facet_width, contrib_len, sub_len, image_width):
    sample_step = sub_len // contrib_len
    centres = jnp.arange(facet_count, dtype=jnp.int32) * facet_width + facet_width // 2
    sample_pos = jnp.arange(contrib_len, dtype=jnp.int32) * sample_step
    cell_ids = jnp.arange(sub_len, dtype=jnp.int32)
    spacing = cell_ids[None, :] - sample_pos[:, None]
    phase_turns = jnp.mod(spacing[None, :, :] * centres[:, None, None], image_width)
    phase_angle = phase_turns.astype(jnp.float32) * (-two_pi / image_width)
    scaled = spacing.astype(jnp.float32) / sample_step
    kernel = 1.0 / (1.0 + scaled * scaled)
    return jnp.stack([jnp.cos(phase_angle) * kernel, jnp.sin(phase_angle) * kernel], 1).astype(jnp.bfloat16)


def reference(slabs, window, density, offsets):
    sample_step = SUB // CONTRIB
    image_width = FACET * FACETS
    blocks = FACETS // 4
    windowed = (slabs.astype(jnp.float32) * window[None, None, None, :]).astype(jnp.bfloat16)
    block_ids = jnp.arange(blocks, dtype=jnp.int32)
    facet_ids = jnp.arange(FACETS, dtype=jnp.int32)

    def encode_facet(facet_id):
        facet_piece = lax.dynamic_slice_in_dim(windowed, facet_id * FACET, FACET, 3).astype(jnp.float32)

        def one_block(block_id):
            phase_table = encode_table(lax.dynamic_slice_in_dim(offsets, block_id * 4, 4, 0), facet_id * FACET, FACET, CONTRIB, sample_step, image_width).astype(jnp.float32)
            raw_prod = jnp.einsum("lpcx,bqjx->lpcbqj", facet_piece, phase_table)
            real_part = raw_prod[:, 0, :, :, 0] - raw_prod[:, 1, :, :, 1]
            imag_part = raw_prod[:, 0, :, :, 1] + raw_prod[:, 1, :, :, 0]
            return jnp.stack([real_part, imag_part], 1)

        pieces = lax.map(one_block, block_ids)
        pieces = jnp.transpose(pieces, (1, 0, 4, 2, 3, 5)).reshape(LAYERS, FACETS, 2, COLS, CONTRIB)
        return (pieces * FACET ** -0.5).astype(jnp.bfloat16)

    encoded = lax.map(encode_facet, facet_ids)
    embed_phase = embed_table(FACETS, FACET, CONTRIB, SUB, image_width).astype(jnp.float32)

    def subgrid_pass(sub_id):
        received = lax.dynamic_index_in_dim(encoded, sub_id, 2, keepdims=False).astype(jnp.float32)
        raw_prod = jnp.einsum("flpcj,fqju->lpcqu", received, embed_phase)
        real_part = raw_prod[:, 0, :, 0] - raw_prod[:, 1, :, 1]
        imag_part = raw_prod[:, 0, :, 1] + raw_prod[:, 1, :, 0]
        counts = lax.dynamic_slice_in_dim(density, sub_id * SUB, SUB, 2)
        weights = jnp.where(counts > 0, 1.0 / jnp.maximum(counts, 1).astype(jnp.float32), jnp.zeros(counts.shape, jnp.float32))
        gridded = (jnp.stack([real_part, imag_part], 1) * weights[:, None] * (2 * FACETS) ** -0.5).astype(jnp.bfloat16)
        raw_back = jnp.einsum("lpcu,fqju->lpcfqj", gridded.astype(jnp.float32), embed_phase)
        real_back = raw_back[:, 0, :, :, 0] + raw_back[:, 1, :, :, 1]
        imag_back = raw_back[:, 1, :, :, 0] - raw_back[:, 0, :, :, 1]
        return (jnp.stack([real_back, imag_back], 1) * 0.5).astype(jnp.bfloat16)

    returned = lax.map(subgrid_pass, facet_ids)

    def adjoint_facet(facet_id):
        row_block = lax.dynamic_index_in_dim(returned, facet_id, 4, keepdims=False)

        def one_block(running, block_id):
            phase_table = encode_table(lax.dynamic_slice_in_dim(offsets, block_id * 4, 4, 0), facet_id * FACET, FACET, CONTRIB, sample_step, image_width).astype(jnp.float32)
            part_rows = lax.dynamic_slice_in_dim(row_block, block_id * 4, 4, 0).astype(jnp.float32)
            raw_prod = jnp.einsum("blpcj,bqjx->lpcqx", part_rows, phase_table)
            real_part = raw_prod[:, 0, :, 0] + raw_prod[:, 1, :, 1]
            imag_part = raw_prod[:, 1, :, 0] - raw_prod[:, 0, :, 1]
            return running + jnp.stack([real_part, imag_part], 1), None

        running, unused = lax.scan(one_block, jnp.zeros((LAYERS, 2, COLS, FACET), jnp.float32), block_ids)
        taper_row = lax.dynamic_slice_in_dim(window, facet_id * FACET, FACET, 0)
        return jnp.sum(running * taper_row * (FACETS * CONTRIB) ** -0.5, axis=0)

    facet_out = lax.map(adjoint_facet, facet_ids)
    return jnp.transpose(facet_out, (1, 2, 0, 3)).reshape(2, COLS, FACETS * FACET)
```

```python
import functools
import math

import jax
import jax.numpy as jnp
from jax import lax
from jax.experimental import pallas as pl
from jax.experimental.pallas import tpu as pltpu
from jax.sharding import PartitionSpec as P

CONTRIB = 128
SUB = 512
GROUP = 4
CHUNK = 512
ROWS = 256
STEP = SUB // CONTRIB

MESH = pl.DeviceIdType.MESH


def sincos(turns, period):
    quarter = jnp.floor(turns.astype(jnp.float32) * (4.0 / period) + 0.5).astype(jnp.int32)
    rest = 4 * turns - quarter * period
    y = rest.astype(jnp.float32) * (0.5 * math.pi / period)
    z = y * y
    s = y + y * z * (-1.0 / 6 + z * (1.0 / 120 + z * (-1.0 / 5040 + z * (1.0 / 362880))))
    c = 1.0 + z * (-0.5 + z * (1.0 / 24 + z * (-1.0 / 720 + z * (1.0 / 40320))))
    odd = (quarter & 1) == 1
    cos_abs = jnp.where(odd, s, c)
    sin_abs = jnp.where(odd, c, s)
    cos_part = jnp.where(((quarter + 1) & 2) == 2, -cos_abs, cos_abs)
    sin_part = jnp.where((quarter & 2) == 2, -sin_abs, sin_abs)
    return cos_part, sin_part


def remainder(value, period):
    return value - jnp.floor(value.astype(jnp.float32) * (1.0 / period)).astype(jnp.int32) * period


def kernel(
    layers, facets, cols, width,
    slab_ref, window_ref, density_ref, offset_ref,
    out_ref,
    wind, ca, sa, table, modulated, acc,
    send1, recv1, embed, kr, ki, rr, ri, raw,
    send2, recv2,
    ssem1, rsem1, ssem2, rsem2,
):
    layer = lax.axis_index("layer")
    me = lax.axis_index("facet")
    rank = layer * facets + me
    total = layers * facets
    image = facets * width
    groups = facets // GROUP
    part = cols // layers

    barrier = pltpu.get_barrier_semaphore()

    def greet(step, carry):
        other = lax.rem(rank + step, total)
        pl.semaphore_signal(
            barrier, inc=1,
            device_id=(other // facets, lax.rem(other, facets)), device_id_type=MESH,
        )
        return carry

    lax.fori_loop(1, total, greet, 0)

    window = window_ref[...]
    for p in range(2):
        wind[p * cols:(p + 1) * cols, :] = (
            (slab_ref[0, p].astype(jnp.float32) * window).astype(jnp.bfloat16).astype(jnp.float32)
        )

    offs = offset_ref[...]
    start = remainder(offs * me, facets) * width
    cell = lax.broadcasted_iota(jnp.int32, (facets, width), 1)
    turns = start + remainder(offs * cell, image)
    cos_a, sin_a = sincos(turns, image)
    ca[...] = cos_a
    sa[...] = sin_a

    lane = lax.broadcasted_iota(jnp.int32, (ROWS, CONTRIB), 1) * STEP
    row = lax.broadcasted_iota(jnp.int32, (ROWS, CONTRIB), 0)
    base_c, base_s = sincos(remainder(lane * me, facets) * width + remainder(lane * row, image), image)
    small = lax.broadcasted_iota(jnp.int32, (8, CONTRIB), 1) * STEP
    for k in range(width // ROWS):
        rot_c, rot_s = sincos(remainder(small * (ROWS * k), image), image)
        rot_c = rot_c[0:1]
        rot_s = rot_s[0:1]
        table[k * ROWS:(k + 1) * ROWS, 0:CONTRIB] = (base_c * rot_c - base_s * rot_s).astype(jnp.bfloat16)
        table[k * ROWS:(k + 1) * ROWS, CONTRIB:2 * CONTRIB] = (
            base_c * rot_s + base_s * rot_c
        ).astype(jnp.bfloat16)

    half = me // (facets // 2)
    half_groups = groups // 2
    scale1 = width ** -0.5

    def encode(step, carry):
        g = lax.rem((1 - half) * half_groups + step, groups)
        for k in range(width // CHUNK):
            xs = slice(k * CHUNK, (k + 1) * CHUNK)
            for t in range(GROUP):
                s = g * GROUP + t
                c_row = ca[pl.ds(s, 1), xs]
                s_row = sa[pl.ds(s, 1), xs]
                wr = wind[0:cols, xs]
                wi = wind[cols:2 * cols, xs]
                lo = t * 2 * cols
                modulated[k % 2, lo:lo + cols, :] = (wr * c_row + wi * s_row).astype(jnp.bfloat16)
                modulated[k % 2, lo + cols:lo + 2 * cols, :] = (wi * c_row - wr * s_row).astype(jnp.bfloat16)
            prod = jnp.dot(modulated[k % 2], table[xs, :], preferred_element_type=jnp.float32)
            if k == 0:
                acc[...] = prod
            else:
                acc[...] += prod
        for t in range(GROUP):
            lo = t * 2 * cols
            pr = acc[lo:lo + cols, :]
            pi = acc[lo + cols:lo + 2 * cols, :]
            real = pr[:, :CONTRIB] + pi[:, CONTRIB:]
            imag = pi[:, :CONTRIB] - pr[:, CONTRIB:]
            send1[g * GROUP + t, 0:cols, :] = (real * scale1).astype(jnp.bfloat16)
            send1[g * GROUP + t, cols:2 * cols, :] = (imag * scale1).astype(jnp.bfloat16)

        @pl.when(step == 0)
        def _():
            pl.semaphore_wait(barrier, total - 1)

        for t in range(GROUP):
            s = g * GROUP + t

            @pl.when(s != me)
            def _():
                pltpu.make_async_remote_copy(
                    src_ref=send1.at[s], dst_ref=recv1.at[me],
                    send_sem=ssem1.at[s], recv_sem=rsem1.at[me],
                    device_id=(layer, s), device_id_type=MESH,
                ).start()

            @pl.when(s == me)
            def _():
                recv1[s] = send1[s]

        return carry

    lax.fori_loop(0, groups, encode, 0)

    spacing = lax.broadcasted_iota(jnp.int32, (CONTRIB, SUB), 1) - STEP * lax.broadcasted_iota(
        jnp.int32, (CONTRIB, SUB), 0
    )
    scaled = spacing.astype(jnp.float32) * (1.0 / STEP)
    weight_k = 1.0 / (1.0 + scaled * scaled)
    c0, s0 = sincos(spacing, 2 * facets)
    kr[...] = c0 * weight_k
    ki[...] = s0 * weight_k
    c1, s1 = sincos(spacing, facets)
    rr[...] = c1
    ri[...] = s1

    def make_embed(f, carry):
        r = kr[...]
        i = ki[...]
        lo = pl.multiple_of(f * CONTRIB, CONTRIB)
        embed[pl.ds(lo, CONTRIB), 0:SUB] = r.astype(jnp.bfloat16)
        embed[pl.ds(lo, CONTRIB), SUB:2 * SUB] = (-i).astype(jnp.bfloat16)
        a = rr[...]
        b = ri[...]
        kr[...] = r * a - i * b
        ki[...] = r * b + i * a
        return carry

    lax.fori_loop(0, facets, make_embed, 0)
    raw[...] = jnp.zeros_like(raw)

    def gather(step, carry):
        g = lax.rem(half * half_groups + step, groups)
        for t in range(GROUP):
            f = g * GROUP + t

            @pl.when(f != me)
            def _():
                pltpu.make_async_remote_copy(
                    src_ref=send1.at[f], dst_ref=recv1.at[f],
                    send_sem=ssem1.at[f], recv_sem=rsem1.at[f],
                    device_id=(layer, f), device_id_type=MESH,
                ).wait()

        lhs = jnp.concatenate([recv1[g * GROUP + t] for t in range(GROUP)], axis=1)
        lo = pl.multiple_of(g * GROUP * CONTRIB, GROUP * CONTRIB)
        raw[...] += jnp.dot(
            lhs, embed[pl.ds(lo, GROUP * CONTRIB), :], preferred_element_type=jnp.float32
        )
        return carry

    lax.fori_loop(0, groups, gather, 0)

    counts = density_ref[0]
    weights = jnp.where(
        counts > 0, 1.0 / jnp.maximum(counts, 1).astype(jnp.float32), 0.0
    )
    sub_scale = (2 * facets) ** -0.5
    raw_r = raw[0:cols, 0:SUB] - raw[cols:2 * cols, SUB:2 * SUB]
    raw_i = raw[0:cols, SUB:2 * SUB] + raw[cols:2 * cols, 0:SUB]
    gridded = jnp.concatenate(
        [
            (raw_r * weights * sub_scale).astype(jnp.bfloat16),
            (raw_i * weights * sub_scale).astype(jnp.bfloat16),
        ],
        axis=0,
    )
    dims = (((1,), (1,)), ((), ()))

    def scatter(step, carry):
        g = lax.rem((1 - half) * half_groups + step, groups)
        lo = pl.multiple_of(g * GROUP * CONTRIB, GROUP * CONTRIB)
        er = embed[pl.ds(lo, GROUP * CONTRIB), 0:SUB]
        ei = embed[pl.ds(lo, GROUP * CONTRIB), SUB:2 * SUB]
        pr = lax.dot_general(gridded, er, dims, preferred_element_type=jnp.float32)
        pi = lax.dot_general(gridded, ei, dims, preferred_element_type=jnp.float32)
        real = ((pr[0:cols] + pi[cols:2 * cols]) * 0.5).astype(jnp.bfloat16)
        imag = ((pr[cols:2 * cols] - pi[0:cols]) * 0.5).astype(jnp.bfloat16)
        for t in range(GROUP):
            f = g * GROUP + t
            js = slice(t * CONTRIB, (t + 1) * CONTRIB)
            for l in range(layers):
                send2[f, l, 0] = real[l * part:(l + 1) * part, js]
                send2[f, l, 1] = imag[l * part:(l + 1) * part, js]
        for t in range(GROUP):
            f = g * GROUP + t
            for l in range(layers):
                own = jnp.logical_and(f == me, layer == l)

                @pl.when(jnp.logical_not(own))
                def _():
                    pltpu.make_async_remote_copy(
                        src_ref=send2.at[f, l], dst_ref=recv2.at[layer, me],
                        send_sem=ssem2.at[l, f], recv_sem=rsem2.at[layer, me],
                        device_id=(l, f), device_id_type=MESH,
                    ).start()

                @pl.when(own)
                def _():
                    recv2[layer, me] = send2[f, l]

        return carry

    lax.fori_loop(0, groups, scatter, 0)

    out_ref[...] = jnp.zeros_like(out_ref)

    def adjoint(step, carry):
        g = lax.rem(half * half_groups + step, groups)
        tops = []
        for t in range(GROUP):
            s = g * GROUP + t
            for l in range(layers):
                own = jnp.logical_and(s == me, layer == l)

                @pl.when(jnp.logical_not(own))
                def _():
                    pltpu.make_async_remote_copy(
                        src_ref=send2.at[s, l], dst_ref=recv2.at[l, s],
                        send_sem=ssem2.at[l, s], recv_sem=rsem2.at[l, s],
                        device_id=(l, s), device_id_type=MESH,
                    ).wait()

        for t in range(GROUP):
            s = g * GROUP + t
            br = recv2[0, s, 0].astype(jnp.float32)
            bi = recv2[0, s, 1].astype(jnp.float32)
            for l in range(1, layers):
                br = br + recv2[l, s, 0].astype(jnp.float32)
                bi = bi + recv2[l, s, 1].astype(jnp.float32)
            tops.append(jnp.concatenate([br, -bi], axis=1))
            tops.append(jnp.concatenate([bi, br], axis=1))
        lhs = jnp.concatenate(tops, axis=0).astype(jnp.bfloat16)
        for k in range(width // CHUNK):
            xs = slice(k * CHUNK, (k + 1) * CHUNK)
            prod = lax.dot_general(lhs, table[xs, :], dims, preferred_element_type=jnp.float32)
            out_r = out_ref[0, :, xs]
            out_i = out_ref[1, :, xs]
            for t in range(GROUP):
                s = g * GROUP + t
                c_row = ca[pl.ds(s, 1), xs]
                s_row = sa[pl.ds(s, 1), xs]
                gr = prod[(2 * t) * part:(2 * t + 1) * part]
                gi = prod[(2 * t + 1) * part:(2 * t + 2) * part]
                out_r = out_r + (c_row * gr - s_row * gi)
                out_i = out_i + (c_row * gi + s_row * gr)
            out_ref[0, :, xs] = out_r
            out_ref[1, :, xs] = out_i
        return carry

    lax.fori_loop(0, groups, adjoint, 0)


def shards(slabs, window, density, offsets):
    facets = lax.axis_size("facet")
    layers = lax.axis_size("layer")
    cols = slabs.shape[2]
    width = slabs.shape[3]
    part = cols // layers
    f32, bf16 = jnp.float32, jnp.bfloat16
    summed = pl.pallas_call(
        functools.partial(kernel, layers, facets, cols, width),
        out_shape=jax.ShapeDtypeStruct((2, part, width), f32),
        in_specs=[pl.BlockSpec(memory_space=pltpu.VMEM)] * 4,
        out_specs=pl.BlockSpec(memory_space=pltpu.VMEM),
        scratch_shapes=[
            pltpu.VMEM((2 * cols, width), f32),
            pltpu.VMEM((facets, width), f32),
            pltpu.VMEM((facets, width), f32),
            pltpu.VMEM((width, 2 * CONTRIB), bf16),
            pltpu.VMEM((2, GROUP * 2 * cols, CHUNK), bf16),
            pltpu.VMEM((GROUP * 2 * cols, 2 * CONTRIB), f32),
            pltpu.VMEM((facets, 2 * cols, CONTRIB), bf16),
            pltpu.VMEM((facets, 2 * cols, CONTRIB), bf16),
            pltpu.VMEM((facets * CONTRIB, 2 * SUB), bf16),
            pltpu.VMEM((CONTRIB, SUB), f32),
            pltpu.VMEM((CONTRIB, SUB), f32),
            pltpu.VMEM((CONTRIB, SUB), f32),
            pltpu.VMEM((CONTRIB, SUB), f32),
            pltpu.VMEM((2 * cols, 2 * SUB), f32),
            pltpu.VMEM((facets, layers, 2, part, CONTRIB), bf16),
            pltpu.VMEM((layers, facets, 2, part, CONTRIB), bf16),
            pltpu.SemaphoreType.DMA((facets,)),
            pltpu.SemaphoreType.DMA((facets,)),
            pltpu.SemaphoreType.DMA((layers, facets)),
            pltpu.SemaphoreType.DMA((layers, facets)),
        ],
        compiler_params=pltpu.CompilerParams(
            collective_id=0, has_side_effects=True, vmem_limit_bytes=56 * 1024 * 1024
        ),
    )(slabs, window[None, :], density, offsets[:, None])
    return summed * (window[None, None, :] * (facets * CONTRIB) ** -0.5)


def solution(mesh):
    placed = (P("layer", None, None, "facet"), P("facet"), P("layer", None, "facet"), P())
    return jax.shard_map(
        shards, mesh=mesh, in_specs=placed, out_specs=P(None, "layer", "facet"), check_vma=False
    )
```

```python
import functools
import math

import jax
import jax.numpy as jnp
from jax import lax
from jax.experimental import pallas as pl
from jax.experimental.pallas import tpu as pltpu
from jax.sharding import PartitionSpec as P

CONTRIB = 128
SUB = 512
GROUP = 4
CHUNK = 512
ROWS = 256
STEP = SUB // CONTRIB

MESH = pl.DeviceIdType.MESH


def sincos(turns, period):
    quarter = jnp.floor(turns.astype(jnp.float32) * (4.0 / period) + 0.5).astype(jnp.int32)
    rest = 4 * turns - quarter * period
    y = rest.astype(jnp.float32) * (0.5 * math.pi / period)
    z = y * y
    s = y + y * z * (-1.0 / 6 + z * (1.0 / 120 + z * (-1.0 / 5040 + z * (1.0 / 362880))))
    c = 1.0 + z * (-0.5 + z * (1.0 / 24 + z * (-1.0 / 720 + z * (1.0 / 40320))))
    odd = (quarter & 1) == 1
    cos_abs = jnp.where(odd, s, c)
    sin_abs = jnp.where(odd, c, s)
    cos_part = jnp.where(((quarter + 1) & 2) == 2, -cos_abs, cos_abs)
    sin_part = jnp.where((quarter & 2) == 2, -sin_abs, sin_abs)
    return cos_part, sin_part


def remainder(value, period):
    return value - jnp.floor(value.astype(jnp.float32) * (1.0 / period)).astype(jnp.int32) * period


def kernel(
    layers, facets, cols, width,
    slab_ref, window_ref, density_ref, offset_ref,
    out_ref,
    slab, counts_ref, window_here, offset_here, wind, ca, sa, table, modulated, acc,
    send1, recv1, embed, kr, ki, rr, ri, raw,
    send2, recv2,
    ssem1, rsem1, ssem2, rsem2, local_sem, up_sem, down_sem, layer_sem,
):
    layer = lax.axis_index("layer")
    me = lax.axis_index("facet")
    image = facets * width
    groups = facets // GROUP
    part = cols // layers
    mine = me // GROUP
    half = mine // (groups // 2)
    half_groups = groups // 2

    def outward(step):
        return jnp.where(
            half == 0,
            lax.rem(half_groups + step, groups),
            lax.rem(half_groups - 1 - step + groups, groups),
        )

    def inward(step):
        return jnp.where(half == 0, step, groups - 1 - step)

    def signal(sem, where):
        pl.semaphore_signal(sem, inc=1, device_id=where, device_id_type=MESH)

    barrier = pltpu.get_barrier_semaphore()
    for o in range(1, layers):
        signal(barrier, (lax.rem(layer + o, layers), me))
    for o in range(1, GROUP):
        signal(barrier, (layer, mine * GROUP + lax.rem(me + o, GROUP)))
    for o in range(GROUP):

        @pl.when(mine > 0)
        def _():
            signal(barrier, (layer, (mine - 1) * GROUP + lax.rem(me + o, GROUP)))

        @pl.when(mine < groups - 1)
        def _():
            signal(barrier, (layer, (mine + 1) * GROUP + lax.rem(me + o, GROUP)))

    fetch_offsets = pltpu.make_async_copy(offset_ref, offset_here, local_sem.at[3])
    fetch_offsets.start()
    fetch_window = pltpu.make_async_copy(window_ref, window_here, local_sem.at[2])
    fetch_window.start()
    fetch_slab = pltpu.make_async_copy(slab_ref, slab, local_sem.at[0])
    fetch_slab.start()
    fetch_counts = pltpu.make_async_copy(density_ref, counts_ref, local_sem.at[1])
    fetch_counts.start()

    def relay(d, wanted_up, wanted_down):
        has_up = mine + d <= groups - 1
        has_down = mine - d >= 0

        @pl.when(jnp.logical_and(has_up, wanted_up))
        def _():
            pl.semaphore_wait(up_sem.at[d], 1)
            if d + 1 < groups:

                @pl.when(mine > 0)
                def _():
                    signal(up_sem.at[d + 1], (layer, me - GROUP))

        @pl.when(jnp.logical_and(has_down, wanted_down))
        def _():
            pl.semaphore_wait(down_sem.at[d], 1)
            if d + 1 < groups:

                @pl.when(mine < groups - 1)
                def _():
                    signal(down_sem.at[d + 1], (layer, me + GROUP))

    first_up = jnp.where(half == 0, half_groups - mine, 1)
    first_down = jnp.where(half == 1, mine - half_groups + 1, 1)

    def meet_near():
        @pl.when(mine == 0)
        def _():
            pl.semaphore_wait(barrier, 2 * GROUP - 1 + layers - 1)

        @pl.when(mine == groups - 1)
        def _():
            pl.semaphore_wait(barrier, 2 * GROUP - 1 + layers - 1)

        @pl.when(jnp.logical_and(mine > 0, mine < groups - 1))
        def _():
            pl.semaphore_wait(barrier, 3 * GROUP - 1 + layers - 1)
            signal(up_sem.at[2], (layer, me - GROUP))
            signal(down_sem.at[2], (layer, me + GROUP))

        for d in range(2, groups):
            relay(d, d <= first_up, d <= first_down)

    def meet_far():
        for d in range(2, groups):
            relay(d, d > first_up, d > first_down)
        for o in range(1, layers):
            signal(layer_sem, (lax.rem(layer + o, layers), me))


    lane = lax.broadcasted_iota(jnp.int32, (ROWS, CONTRIB), 1) * STEP
    row = lax.broadcasted_iota(jnp.int32, (ROWS, CONTRIB), 0)
    base_c, base_s = sincos(remainder(lane * me, facets) * width + remainder(lane * row, image), image)
    small = lax.broadcasted_iota(jnp.int32, (8, CONTRIB), 1) * STEP
    for k in range(width // ROWS):
        rot_c, rot_s = sincos(remainder(small * (ROWS * k), image), image)
        rot_c = rot_c[0:1]
        rot_s = rot_s[0:1]
        table[k * ROWS:(k + 1) * ROWS, 0:CONTRIB] = (base_c * rot_c - base_s * rot_s).astype(jnp.bfloat16)
        table[k * ROWS:(k + 1) * ROWS, CONTRIB:2 * CONTRIB] = (
            base_c * rot_s + base_s * rot_c
        ).astype(jnp.bfloat16)

    fetch_offsets.wait()
    square = (GROUP * groups, GROUP * groups)
    on_diagonal = lax.broadcasted_iota(jnp.int32, square, 0) == lax.broadcasted_iota(jnp.int32, square, 1)
    offs = jnp.sum(
        jnp.where(on_diagonal, offset_here[...].astype(jnp.float32), 0.0), axis=1, keepdims=True
    ).astype(jnp.int32)
    start = remainder(offs * me, facets) * width
    cell = lax.broadcasted_iota(jnp.int32, (facets, width), 1)
    turns = start + remainder(offs * cell, image)
    cos_a, sin_a = sincos(turns, image)
    ca[...] = cos_a
    sa[...] = sin_a

    fetch_window.wait()
    fetch_slab.wait()
    window = window_here[...]
    for p in range(2):
        wind[p * cols:(p + 1) * cols, :] = (
            (slab[0, p].astype(jnp.float32) * window).astype(jnp.bfloat16).astype(jnp.float32)
        )

    scale1 = width ** -0.5

    def encode(step, carry):
        g = outward(step)
        for k in range(width // CHUNK):
            xs = slice(k * CHUNK, (k + 1) * CHUNK)
            for t in range(GROUP):
                s = g * GROUP + t
                c_row = ca[pl.ds(s, 1), xs]
                s_row = sa[pl.ds(s, 1), xs]
                wr = wind[0:cols, xs]
                wi = wind[cols:2 * cols, xs]
                lo = t * 2 * cols
                modulated[k % 2, lo:lo + cols, :] = (wr * c_row + wi * s_row).astype(jnp.bfloat16)
                modulated[k % 2, lo + cols:lo + 2 * cols, :] = (wi * c_row - wr * s_row).astype(jnp.bfloat16)
            prod = jnp.dot(modulated[k % 2], table[xs, :], preferred_element_type=jnp.float32)
            if k == 0:
                acc[...] = prod
            else:
                acc[...] += prod
        for t in range(GROUP):
            lo = t * 2 * cols
            pr = acc[lo:lo + cols, :]
            pi = acc[lo + cols:lo + 2 * cols, :]
            real = pr[:, :CONTRIB] + pi[:, CONTRIB:]
            imag = pi[:, :CONTRIB] - pr[:, CONTRIB:]
            send1[g * GROUP + t, 0:cols, :] = (real * scale1).astype(jnp.bfloat16)
            send1[g * GROUP + t, cols:2 * cols, :] = (imag * scale1).astype(jnp.bfloat16)

        @pl.when(step == 0)
        def _():
            meet_near()

        @pl.when(step == 1)
        def _():
            meet_far()

        for t in range(GROUP):
            s = g * GROUP + t

            @pl.when(s != me)
            def _():
                pltpu.make_async_remote_copy(
                    src_ref=send1.at[s], dst_ref=recv1.at[me],
                    send_sem=ssem1.at[s], recv_sem=rsem1.at[me],
                    device_id=(layer, s), device_id_type=MESH,
                ).start()

            @pl.when(s == me)
            def _():
                recv1[s] = send1[s]

        return carry

    lax.fori_loop(0, groups, encode, 0)

    spacing = lax.broadcasted_iota(jnp.int32, (CONTRIB, SUB), 1) - STEP * lax.broadcasted_iota(
        jnp.int32, (CONTRIB, SUB), 0
    )
    scaled = spacing.astype(jnp.float32) * (1.0 / STEP)
    weight_k = 1.0 / (1.0 + scaled * scaled)
    c0, s0 = sincos(spacing, 2 * facets)
    kr[...] = c0 * weight_k
    ki[...] = s0 * weight_k
    c1, s1 = sincos(spacing, facets)
    rr[...] = c1
    ri[...] = s1

    def make_embed(f, carry):
        r = kr[...]
        i = ki[...]
        lo = pl.multiple_of(f * CONTRIB, CONTRIB)
        embed[pl.ds(lo, CONTRIB), 0:SUB] = r.astype(jnp.bfloat16)
        embed[pl.ds(lo, CONTRIB), SUB:2 * SUB] = (-i).astype(jnp.bfloat16)
        a = rr[...]
        b = ri[...]
        kr[...] = r * a - i * b
        ki[...] = r * b + i * a
        return carry

    lax.fori_loop(0, facets, make_embed, 0)
    raw[...] = jnp.zeros_like(raw)

    def gather(step, carry):
        g = inward(step)
        for t in range(GROUP):
            f = g * GROUP + t

            @pl.when(f != me)
            def _():
                pltpu.make_async_remote_copy(
                    src_ref=send1.at[f], dst_ref=recv1.at[f],
                    send_sem=ssem1.at[f], recv_sem=rsem1.at[f],
                    device_id=(layer, f), device_id_type=MESH,
                ).wait()

        lhs = jnp.concatenate([recv1[g * GROUP + t] for t in range(GROUP)], axis=1)
        lo = pl.multiple_of(g * GROUP * CONTRIB, GROUP * CONTRIB)
        raw[...] += jnp.dot(
            lhs, embed[pl.ds(lo, GROUP * CONTRIB), :], preferred_element_type=jnp.float32
        )
        return carry

    lax.fori_loop(0, groups, gather, 0)

    fetch_counts.wait()
    counts = counts_ref[0]
    weights = jnp.where(
        counts > 0, 1.0 / jnp.maximum(counts, 1).astype(jnp.float32), 0.0
    )
    sub_scale = (2 * facets) ** -0.5
    raw_r = raw[0:cols, 0:SUB] - raw[cols:2 * cols, SUB:2 * SUB]
    raw_i = raw[0:cols, SUB:2 * SUB] + raw[cols:2 * cols, 0:SUB]
    gridded = jnp.concatenate(
        [
            (raw_r * weights * sub_scale).astype(jnp.bfloat16),
            (raw_i * weights * sub_scale).astype(jnp.bfloat16),
        ],
        axis=0,
    )
    dims = (((1,), (1,)), ((), ()))

    pl.semaphore_wait(layer_sem, layers - 1)

    def scatter(step, carry):
        g = outward(step)
        lo = pl.multiple_of(g * GROUP * CONTRIB, GROUP * CONTRIB)
        er = embed[pl.ds(lo, GROUP * CONTRIB), 0:SUB]
        ei = embed[pl.ds(lo, GROUP * CONTRIB), SUB:2 * SUB]
        pr = lax.dot_general(gridded, er, dims, preferred_element_type=jnp.float32)
        pi = lax.dot_general(gridded, ei, dims, preferred_element_type=jnp.float32)
        real = ((pr[0:cols] + pi[cols:2 * cols]) * 0.5).astype(jnp.bfloat16)
        imag = ((pr[cols:2 * cols] - pi[0:cols]) * 0.5).astype(jnp.bfloat16)
        for t in range(GROUP):
            f = g * GROUP + t
            js = slice(t * CONTRIB, (t + 1) * CONTRIB)
            for l in range(layers):
                send2[f, l, 0] = real[l * part:(l + 1) * part, js]
                send2[f, l, 1] = imag[l * part:(l + 1) * part, js]
        for t in range(GROUP):
            f = g * GROUP + t
            for l in range(layers):
                own = jnp.logical_and(f == me, layer == l)

                @pl.when(jnp.logical_not(own))
                def _():
                    pltpu.make_async_remote_copy(
                        src_ref=send2.at[f, l], dst_ref=recv2.at[layer, me],
                        send_sem=ssem2.at[l, f], recv_sem=rsem2.at[layer, me],
                        device_id=(l, f), device_id_type=MESH,
                    ).start()

                @pl.when(own)
                def _():
                    recv2[layer, me] = send2[f, l]

        return carry

    lax.fori_loop(0, groups, scatter, 0)

    out_ref[...] = jnp.zeros_like(out_ref)

    def adjoint(step, carry):
        g = inward(step)
        tops = []
        for t in range(GROUP):
            s = g * GROUP + t
            for l in range(layers):
                own = jnp.logical_and(s == me, layer == l)

                @pl.when(jnp.logical_not(own))
                def _():
                    pltpu.make_async_remote_copy(
                        src_ref=send2.at[s, l], dst_ref=recv2.at[l, s],
                        send_sem=ssem2.at[l, s], recv_sem=rsem2.at[l, s],
                        device_id=(l, s), device_id_type=MESH,
                    ).wait()

        for t in range(GROUP):
            s = g * GROUP + t
            br = recv2[0, s, 0].astype(jnp.float32)
            bi = recv2[0, s, 1].astype(jnp.float32)
            for l in range(1, layers):
                br = br + recv2[l, s, 0].astype(jnp.float32)
                bi = bi + recv2[l, s, 1].astype(jnp.float32)
            tops.append(jnp.concatenate([br, -bi], axis=1))
            tops.append(jnp.concatenate([bi, br], axis=1))
        lhs = jnp.concatenate(tops, axis=0).astype(jnp.bfloat16)
        for k in range(width // CHUNK):
            xs = slice(k * CHUNK, (k + 1) * CHUNK)
            prod = lax.dot_general(lhs, table[xs, :], dims, preferred_element_type=jnp.float32)
            out_r = out_ref[0, :, xs]
            out_i = out_ref[1, :, xs]
            for t in range(GROUP):
                s = g * GROUP + t
                c_row = ca[pl.ds(s, 1), xs]
                s_row = sa[pl.ds(s, 1), xs]
                gr = prod[(2 * t) * part:(2 * t + 1) * part]
                gi = prod[(2 * t + 1) * part:(2 * t + 2) * part]
                out_r = out_r + (c_row * gr - s_row * gi)
                out_i = out_i + (c_row * gi + s_row * gr)
            out_ref[0, :, xs] = out_r
            out_ref[1, :, xs] = out_i
        return carry

    lax.fori_loop(0, groups, adjoint, 0)


def shards(slabs, window, density, offsets):
    facets = lax.axis_size("facet")
    layers = lax.axis_size("layer")
    cols = slabs.shape[2]
    width = slabs.shape[3]
    part = cols // layers
    f32, bf16 = jnp.float32, jnp.bfloat16
    summed = pl.pallas_call(
        functools.partial(kernel, layers, facets, cols, width),
        out_shape=jax.ShapeDtypeStruct((2, part, width), f32),
        in_specs=[pl.BlockSpec(memory_space=pltpu.HBM)] * 4,
        out_specs=pl.BlockSpec(memory_space=pltpu.VMEM),
        scratch_shapes=[
            pltpu.VMEM(slabs.shape, bf16),
            pltpu.VMEM(density.shape, jnp.int32),
            pltpu.VMEM((1, width), f32),
            pltpu.VMEM((1, facets), jnp.int32),
            pltpu.VMEM((2 * cols, width), f32),
            pltpu.VMEM((facets, width), f32),
            pltpu.VMEM((facets, width), f32),
            pltpu.VMEM((width, 2 * CONTRIB), bf16),
            pltpu.VMEM((2, GROUP * 2 * cols, CHUNK), bf16),
            pltpu.VMEM((GROUP * 2 * cols, 2 * CONTRIB), f32),
            pltpu.VMEM((facets, 2 * cols, CONTRIB), bf16),
            pltpu.VMEM((facets, 2 * cols, CONTRIB), bf16),
            pltpu.VMEM((facets * CONTRIB, 2 * SUB), bf16),
            pltpu.VMEM((CONTRIB, SUB), f32),
            pltpu.VMEM((CONTRIB, SUB), f32),
            pltpu.VMEM((CONTRIB, SUB), f32),
            pltpu.VMEM((CONTRIB, SUB), f32),
            pltpu.VMEM((2 * cols, 2 * SUB), f32),
            pltpu.VMEM((facets, layers, 2, part, CONTRIB), bf16),
            pltpu.VMEM((layers, facets, 2, part, CONTRIB), bf16),
            pltpu.SemaphoreType.DMA((facets,)),
            pltpu.SemaphoreType.DMA((facets,)),
            pltpu.SemaphoreType.DMA((layers, facets)),
            pltpu.SemaphoreType.DMA((layers, facets)),
            pltpu.SemaphoreType.DMA((4,)),
            pltpu.SemaphoreType.REGULAR((facets // GROUP,)),
            pltpu.SemaphoreType.REGULAR((facets // GROUP,)),
            pltpu.SemaphoreType.REGULAR,
        ],
        compiler_params=pltpu.CompilerParams(
            collective_id=0, has_side_effects=True, vmem_limit_bytes=(14 + facets) * 1024 * 1024
        ),
    )(slabs, window[None, :], density, offsets[None, :])
    return summed * (window[None, None, :] * (facets * CONTRIB) ** -0.5)


def solution(mesh):
    placed = (P("layer", None, None, "facet"), P("facet"), P("layer", None, "facet"), P())
    return jax.shard_map(
        shards, mesh=mesh, in_specs=placed, out_specs=P(None, "layer", "facet"), check_vma=False
    )
```

```python
import functools
import math

import jax
import jax.numpy as jnp
from jax import lax
from jax.experimental import pallas as pl
from jax.experimental.pallas import tpu as pltpu
from jax.sharding import PartitionSpec as P

CONTRIB = 128
SUB = 512
GROUP = 4
CHUNK = 512
ROWS = 256
STEP = SUB // CONTRIB

MESH = pl.DeviceIdType.MESH


def sincos(turns, period):
    quarter = jnp.floor(turns.astype(jnp.float32) * (4.0 / period) + 0.5).astype(jnp.int32)
    rest = 4 * turns - quarter * period
    y = rest.astype(jnp.float32) * (0.5 * math.pi / period)
    z = y * y
    s = y + y * z * (-1.0 / 6 + z * (1.0 / 120 + z * (-1.0 / 5040 + z * (1.0 / 362880))))
    c = 1.0 + z * (-0.5 + z * (1.0 / 24 + z * (-1.0 / 720 + z * (1.0 / 40320))))
    odd = (quarter & 1) == 1
    cos_abs = jnp.where(odd, s, c)
    sin_abs = jnp.where(odd, c, s)
    cos_part = jnp.where(((quarter + 1) & 2) == 2, -cos_abs, cos_abs)
    sin_part = jnp.where((quarter & 2) == 2, -sin_abs, sin_abs)
    return cos_part, sin_part


def remainder(value, period):
    return value - jnp.floor(value.astype(jnp.float32) * (1.0 / period)).astype(jnp.int32) * period


def kernel(
    layers, facets, cols, width,
    slab_ref, window_ref, density_ref, offset_ref,
    out_ref,
    slab, counts_ref, window_here, offset_here, wind, ca, sa, table, modulated, acc,
    send1, recv1, embed, kr, ki, rr, ri, raw,
    send2, recv2,
    ssem1, rsem1, ssem2, rsem2, local_sem, up_sem, down_sem, layer_sem,
):
    layer = lax.axis_index("layer")
    me = lax.axis_index("facet")
    image = facets * width
    groups = facets // GROUP
    part = cols // layers
    mine = me // GROUP
    half = mine // (groups // 2)
    half_groups = groups // 2

    def outward(step):
        return jnp.where(
            half == 0,
            lax.rem(half_groups + step, groups),
            lax.rem(half_groups - 1 - step + groups, groups),
        )

    def inward(step):
        return jnp.where(half == 0, step, groups - 1 - step)

    def signal(sem, where):
        pl.semaphore_signal(sem, inc=1, device_id=where, device_id_type=MESH)

    barrier = pltpu.get_barrier_semaphore()
    for o in range(1, layers):
        signal(barrier, (lax.rem(layer + o, layers), me))
    for o in range(1, GROUP):
        signal(barrier, (layer, mine * GROUP + lax.rem(me + o, GROUP)))
    for o in range(GROUP):

        @pl.when(mine > 0)
        def _():
            signal(barrier, (layer, (mine - 1) * GROUP + lax.rem(me + o, GROUP)))

        @pl.when(mine < groups - 1)
        def _():
            signal(barrier, (layer, (mine + 1) * GROUP + lax.rem(me + o, GROUP)))

    fetch_offsets = pltpu.make_async_copy(offset_ref, offset_here, local_sem.at[3])
    fetch_offsets.start()
    fetch_window = pltpu.make_async_copy(window_ref, window_here, local_sem.at[2])
    fetch_window.start()
    fetch_slab = pltpu.make_async_copy(slab_ref, slab, local_sem.at[0])
    fetch_slab.start()
    fetch_counts = pltpu.make_async_copy(density_ref, counts_ref, local_sem.at[1])
    fetch_counts.start()

    def relay(d, wanted_up, wanted_down):
        has_up = mine + d <= groups - 1
        has_down = mine - d >= 0

        @pl.when(jnp.logical_and(has_up, wanted_up))
        def _():
            pl.semaphore_wait(up_sem.at[d], 1)
            if d + 1 < groups:

                @pl.when(mine > 0)
                def _():
                    signal(up_sem.at[d + 1], (layer, me - GROUP))

        @pl.when(jnp.logical_and(has_down, wanted_down))
        def _():
            pl.semaphore_wait(down_sem.at[d], 1)
            if d + 1 < groups:

                @pl.when(mine < groups - 1)
                def _():
                    signal(down_sem.at[d + 1], (layer, me + GROUP))

    first_up = jnp.where(half == 0, half_groups - mine, 1)
    first_down = jnp.where(half == 1, mine - half_groups + 1, 1)

    def meet_near():
        @pl.when(mine == 0)
        def _():
            pl.semaphore_wait(barrier, 2 * GROUP - 1 + layers - 1)

        @pl.when(mine == groups - 1)
        def _():
            pl.semaphore_wait(barrier, 2 * GROUP - 1 + layers - 1)

        @pl.when(jnp.logical_and(mine > 0, mine < groups - 1))
        def _():
            pl.semaphore_wait(barrier, 3 * GROUP - 1 + layers - 1)
            signal(up_sem.at[2], (layer, me - GROUP))
            signal(down_sem.at[2], (layer, me + GROUP))

        for d in range(2, groups):
            relay(d, d <= first_up, d <= first_down)

    def meet_far():
        for d in range(2, groups):
            relay(d, d > first_up, d > first_down)
        for o in range(1, layers):
            signal(layer_sem, (lax.rem(layer + o, layers), me))


    lane = lax.broadcasted_iota(jnp.int32, (ROWS, CONTRIB), 1) * STEP
    row = lax.broadcasted_iota(jnp.int32, (ROWS, CONTRIB), 0)
    base_c, base_s = sincos(remainder(lane * me, facets) * width + remainder(lane * row, image), image)
    small = lax.broadcasted_iota(jnp.int32, (8, CONTRIB), 1) * STEP
    for k in range(width // ROWS):
        rot_c, rot_s = sincos(remainder(small * (ROWS * k), image), image)
        rot_c = rot_c[0:1]
        rot_s = rot_s[0:1]
        table[k * ROWS:(k + 1) * ROWS, 0:CONTRIB] = (base_c * rot_c - base_s * rot_s).astype(jnp.bfloat16)
        table[k * ROWS:(k + 1) * ROWS, CONTRIB:2 * CONTRIB] = (
            base_c * rot_s + base_s * rot_c
        ).astype(jnp.bfloat16)

    fetch_offsets.wait()
    square = (GROUP * groups, GROUP * groups)
    on_diagonal = lax.broadcasted_iota(jnp.int32, square, 0) == lax.broadcasted_iota(jnp.int32, square, 1)
    offs = jnp.sum(
        jnp.where(on_diagonal, offset_here[...].astype(jnp.float32), 0.0), axis=1, keepdims=True
    ).astype(jnp.int32)
    start = remainder(offs * me, facets) * width
    cell = lax.broadcasted_iota(jnp.int32, (facets, width), 1)
    turns = start + remainder(offs * cell, image)
    cos_a, sin_a = sincos(turns, image)
    ca[...] = cos_a
    sa[...] = sin_a

    fetch_window.wait()
    fetch_slab.wait()
    window = window_here[...]
    for p in range(2):
        wind[p * cols:(p + 1) * cols, :] = (
            (slab[0, p].astype(jnp.float32) * window).astype(jnp.bfloat16).astype(jnp.float32)
        )

    scale1 = width ** -0.5

    def encode(step, carry):
        g = outward(step)
        for k in range(width // CHUNK):
            xs = slice(k * CHUNK, (k + 1) * CHUNK)
            for t in range(GROUP):
                s = g * GROUP + t
                c_row = ca[pl.ds(s, 1), xs]
                s_row = sa[pl.ds(s, 1), xs]
                wr = wind[0:cols, xs]
                wi = wind[cols:2 * cols, xs]
                lo = t * 2 * cols
                modulated[k % 2, lo:lo + cols, :] = (wr * c_row + wi * s_row).astype(jnp.bfloat16)
                modulated[k % 2, lo + cols:lo + 2 * cols, :] = (wi * c_row - wr * s_row).astype(jnp.bfloat16)
            prod = jnp.dot(modulated[k % 2], table[xs, :], preferred_element_type=jnp.float32)
            if k == 0:
                acc[...] = prod
            else:
                acc[...] += prod
        for t in range(GROUP):
            lo = t * 2 * cols
            pr = acc[lo:lo + cols, :]
            pi = acc[lo + cols:lo + 2 * cols, :]
            real = pr[:, :CONTRIB] + pi[:, CONTRIB:]
            imag = pi[:, :CONTRIB] - pr[:, CONTRIB:]
            send1[g * GROUP + t, 0:cols, :] = (real * scale1).astype(jnp.bfloat16)
            send1[g * GROUP + t, cols:2 * cols, :] = (imag * scale1).astype(jnp.bfloat16)

        @pl.when(step == 0)
        def _():
            meet_near()

        @pl.when(step == 1)
        def _():
            meet_far()

        for t in range(GROUP):
            s = g * GROUP + t

            @pl.when(s != me)
            def _():
                pltpu.make_async_remote_copy(
                    src_ref=send1.at[s], dst_ref=recv1.at[me],
                    send_sem=ssem1.at[s], recv_sem=rsem1.at[me],
                    device_id=(layer, s), device_id_type=MESH,
                ).start()

            @pl.when(s == me)
            def _():
                recv1[s] = send1[s]

        return carry

    lax.fori_loop(0, groups, encode, 0)

    spacing = lax.broadcasted_iota(jnp.int32, (CONTRIB, SUB), 1) - STEP * lax.broadcasted_iota(
        jnp.int32, (CONTRIB, SUB), 0
    )
    scaled = spacing.astype(jnp.float32) * (1.0 / STEP)
    weight_k = 1.0 / (1.0 + scaled * scaled)
    c0, s0 = sincos(spacing, 2 * facets)
    kr[...] = c0 * weight_k
    ki[...] = s0 * weight_k
    c1, s1 = sincos(spacing, facets)
    rr[...] = c1
    ri[...] = s1

    def make_embed(f, carry):
        r = kr[...]
        i = ki[...]
        lo = pl.multiple_of(f * CONTRIB, CONTRIB)
        embed[pl.ds(lo, CONTRIB), 0:SUB] = r.astype(jnp.bfloat16)
        embed[pl.ds(lo, CONTRIB), SUB:2 * SUB] = (-i).astype(jnp.bfloat16)
        a = rr[...]
        b = ri[...]
        kr[...] = r * a - i * b
        ki[...] = r * b + i * a
        return carry

    lax.fori_loop(0, facets, make_embed, 0)
    raw[...] = jnp.zeros_like(raw)

    def gather(step, carry):
        g = inward(step)
        for t in range(GROUP):
            f = g * GROUP + t

            @pl.when(f != me)
            def _():
                pltpu.make_async_remote_copy(
                    src_ref=send1.at[f], dst_ref=recv1.at[f],
                    send_sem=ssem1.at[f], recv_sem=rsem1.at[f],
                    device_id=(layer, f), device_id_type=MESH,
                ).wait()

        lhs = jnp.concatenate([recv1[g * GROUP + t] for t in range(GROUP)], axis=1)
        lo = pl.multiple_of(g * GROUP * CONTRIB, GROUP * CONTRIB)
        raw[...] += jnp.dot(
            lhs, embed[pl.ds(lo, GROUP * CONTRIB), :], preferred_element_type=jnp.float32
        )
        return carry

    lax.fori_loop(0, groups, gather, 0)

    fetch_counts.wait()
    counts = counts_ref[0]
    weights = jnp.where(
        counts > 0, 1.0 / jnp.maximum(counts, 1).astype(jnp.float32), 0.0
    )
    sub_scale = (2 * facets) ** -0.5
    raw_r = raw[0:cols, 0:SUB] - raw[cols:2 * cols, SUB:2 * SUB]
    raw_i = raw[0:cols, SUB:2 * SUB] + raw[cols:2 * cols, 0:SUB]
    gridded = jnp.concatenate(
        [
            (raw_r * weights * sub_scale).astype(jnp.bfloat16),
            (raw_i * weights * sub_scale).astype(jnp.bfloat16),
        ],
        axis=0,
    )
    dims = (((1,), (1,)), ((), ()))

    pl.semaphore_wait(layer_sem, layers - 1)

    def scatter(step, carry):
        g = outward(step)
        lo = pl.multiple_of(g * GROUP * CONTRIB, GROUP * CONTRIB)
        er = embed[pl.ds(lo, GROUP * CONTRIB), 0:SUB]
        ei = embed[pl.ds(lo, GROUP * CONTRIB), SUB:2 * SUB]
        pr = lax.dot_general(gridded, er, dims, preferred_element_type=jnp.float32)
        pi = lax.dot_general(gridded, ei, dims, preferred_element_type=jnp.float32)
        real = ((pr[0:cols] + pi[cols:2 * cols]) * 0.5).astype(jnp.bfloat16)
        imag = ((pr[cols:2 * cols] - pi[0:cols]) * 0.5).astype(jnp.bfloat16)
        for t in range(GROUP):
            f = g * GROUP + t
            js = slice(t * CONTRIB, (t + 1) * CONTRIB)
            for l in range(layers):
                send2[f, l, 0] = real[l * part:(l + 1) * part, js]
                send2[f, l, 1] = imag[l * part:(l + 1) * part, js]
        for t in range(GROUP):
            f = g * GROUP + t
            for l in range(layers):
                own = jnp.logical_and(f == me, layer == l)

                @pl.when(jnp.logical_not(own))
                def _():
                    pltpu.make_async_remote_copy(
                        src_ref=send2.at[f, l], dst_ref=recv2.at[layer, me],
                        send_sem=ssem2.at[l, f], recv_sem=rsem2.at[layer, me],
                        device_id=(l, f), device_id_type=MESH,
                    ).start()

                @pl.when(own)
                def _():
                    recv2[layer, me] = send2[f, l]

        return carry

    lax.fori_loop(0, groups, scatter, 0)

    out_ref[...] = jnp.zeros_like(out_ref)

    def adjoint(step, carry):
        g = inward(step)
        tops = []
        for t in range(GROUP):
            s = g * GROUP + t
            for l in range(layers):
                own = jnp.logical_and(s == me, layer == l)

                @pl.when(jnp.logical_not(own))
                def _():
                    pltpu.make_async_remote_copy(
                        src_ref=send2.at[s, l], dst_ref=recv2.at[l, s],
                        send_sem=ssem2.at[l, s], recv_sem=rsem2.at[l, s],
                        device_id=(l, s), device_id_type=MESH,
                    ).wait()

        for t in range(GROUP):
            s = g * GROUP + t
            br = recv2[0, s, 0].astype(jnp.float32)
            bi = recv2[0, s, 1].astype(jnp.float32)
            for l in range(1, layers):
                br = br + recv2[l, s, 0].astype(jnp.float32)
                bi = bi + recv2[l, s, 1].astype(jnp.float32)
            tops.append(jnp.concatenate([br, -bi], axis=1))
            tops.append(jnp.concatenate([bi, br], axis=1))
        lhs = jnp.concatenate(tops, axis=0).astype(jnp.bfloat16)
        for k in range(width // CHUNK):
            xs = slice(k * CHUNK, (k + 1) * CHUNK)
            prod = lax.dot_general(lhs, table[xs, :], dims, preferred_element_type=jnp.float32)
            out_r = out_ref[0, :, xs]
            out_i = out_ref[1, :, xs]
            for t in range(GROUP):
                s = g * GROUP + t
                c_row = ca[pl.ds(s, 1), xs]
                s_row = sa[pl.ds(s, 1), xs]
                gr = prod[(2 * t) * part:(2 * t + 1) * part]
                gi = prod[(2 * t + 1) * part:(2 * t + 2) * part]
                out_r = out_r + (c_row * gr - s_row * gi)
                out_i = out_i + (c_row * gi + s_row * gr)
            out_ref[0, :, xs] = out_r
            out_ref[1, :, xs] = out_i
        return carry

    lax.fori_loop(0, groups, adjoint, 0)


def shards(slabs, window, density, offsets):
    facets = lax.axis_size("facet")
    layers = lax.axis_size("layer")
    cols = slabs.shape[2]
    width = slabs.shape[3]
    part = cols // layers
    f32, bf16 = jnp.float32, jnp.bfloat16
    summed = pl.pallas_call(
        functools.partial(kernel, layers, facets, cols, width),
        out_shape=jax.ShapeDtypeStruct((2, part, width), f32),
        in_specs=[pl.BlockSpec(memory_space=pltpu.HBM)] * 4,
        out_specs=pl.BlockSpec(memory_space=pltpu.VMEM),
        scratch_shapes=[
            pltpu.VMEM(slabs.shape, bf16),
            pltpu.VMEM(density.shape, jnp.int32),
            pltpu.VMEM((1, width), f32),
            pltpu.VMEM((1, facets), jnp.int32),
            pltpu.VMEM((2 * cols, width), f32),
            pltpu.VMEM((facets, width), f32),
            pltpu.VMEM((facets, width), f32),
            pltpu.VMEM((width, 2 * CONTRIB), bf16),
            pltpu.VMEM((2, GROUP * 2 * cols, CHUNK), bf16),
            pltpu.VMEM((GROUP * 2 * cols, 2 * CONTRIB), f32),
            pltpu.VMEM((facets, 2 * cols, CONTRIB), bf16),
            pltpu.VMEM((facets, 2 * cols, CONTRIB), bf16),
            pltpu.VMEM((facets * CONTRIB, 2 * SUB), bf16),
            pltpu.VMEM((CONTRIB, SUB), f32),
            pltpu.VMEM((CONTRIB, SUB), f32),
            pltpu.VMEM((CONTRIB, SUB), f32),
            pltpu.VMEM((CONTRIB, SUB), f32),
            pltpu.VMEM((2 * cols, 2 * SUB), f32),
            pltpu.VMEM((facets, layers, 2, part, CONTRIB), bf16),
            pltpu.VMEM((layers, facets, 2, part, CONTRIB), bf16),
            pltpu.SemaphoreType.DMA((facets,)),
            pltpu.SemaphoreType.DMA((facets,)),
            pltpu.SemaphoreType.DMA((layers, facets)),
            pltpu.SemaphoreType.DMA((layers, facets)),
            pltpu.SemaphoreType.DMA((4,)),
            pltpu.SemaphoreType.REGULAR((facets // GROUP,)),
            pltpu.SemaphoreType.REGULAR((facets // GROUP,)),
            pltpu.SemaphoreType.REGULAR,
        ],
        compiler_params=pltpu.CompilerParams(
            collective_id=0, has_side_effects=True, vmem_limit_bytes=(14 + facets) * 1024 * 1024
        ),
    )(
        *(
            pltpu.with_memory_space_constraint(x, pltpu.HBM)
            for x in (slabs, window[None, :], density, offsets[None, :])
        )
    )
    return summed * (facets * CONTRIB) ** -0.5 * window[None, None, :]


def solution(mesh):
    placed = (P("layer", None, None, "facet"), P("facet"), P("layer", None, "facet"), P())
    return jax.shard_map(
        shards, mesh=mesh, in_specs=placed, out_specs=P(None, "layer", "facet"), check_vma=False
    )
```

```python
import functools
import math

import jax
import jax.numpy as jnp
from jax import lax
from jax.experimental import pallas as pl
from jax.experimental.pallas import tpu as pltpu
from jax.sharding import PartitionSpec as P

CONTRIB = 128
SUB = 512
GROUP = 4
CHUNK = 512
ROWS = 256
STEP = SUB // CONTRIB

MESH = pl.DeviceIdType.MESH


def sincos(turns, period):
    quarter = jnp.floor(turns.astype(jnp.float32) * (4.0 / period) + 0.5).astype(jnp.int32)
    rest = 4 * turns - quarter * period
    y = rest.astype(jnp.float32) * (0.5 * math.pi / period)
    z = y * y
    s = y + y * z * (-1.0 / 6 + z * (1.0 / 120 + z * (-1.0 / 5040 + z * (1.0 / 362880))))
    c = 1.0 + z * (-0.5 + z * (1.0 / 24 + z * (-1.0 / 720 + z * (1.0 / 40320))))
    odd = (quarter & 1) == 1
    cos_abs = jnp.where(odd, s, c)
    sin_abs = jnp.where(odd, c, s)
    cos_part = jnp.where(((quarter + 1) & 2) == 2, -cos_abs, cos_abs)
    sin_part = jnp.where((quarter & 2) == 2, -sin_abs, sin_abs)
    return cos_part, sin_part


def remainder(value, period):
    return value - jnp.floor(value.astype(jnp.float32) * (1.0 / period)).astype(jnp.int32) * period


def kernel(
    layers, facets, cols, width,
    slab_ref, window_ref, density_ref, offset_ref,
    out_ref,
    slab, counts_ref, window_here, offset_here, wind, ca, sa, table, modulated, acc,
    send1, recv1, embed, kr, ki, rr, ri, raw,
    send2, recv2,
    ssem1, rsem1, ssem2, rsem2, local_sem, up_sem, down_sem, layer_sem,
):
    layer = lax.axis_index("layer")
    me = lax.axis_index("facet")
    image = facets * width
    groups = facets // GROUP
    part = cols // layers
    mine = me // GROUP
    half = mine // (groups // 2)
    half_groups = groups // 2

    def outward(step):
        return jnp.where(
            half == 0,
            lax.rem(half_groups + step, groups),
            lax.rem(half_groups - 1 - step + groups, groups),
        )

    def inward(step):
        return jnp.where(half == 0, step, groups - 1 - step)

    def signal(sem, where):
        pl.semaphore_signal(sem, inc=1, device_id=where, device_id_type=MESH)

    barrier = pltpu.get_barrier_semaphore()
    for o in range(1, layers):
        signal(barrier, (lax.rem(layer + o, layers), me))
    for o in range(1, GROUP):
        signal(barrier, (layer, mine * GROUP + lax.rem(me + o, GROUP)))
    for o in range(GROUP):

        @pl.when(mine > 0)
        def _():
            signal(barrier, (layer, (mine - 1) * GROUP + lax.rem(me + o, GROUP)))

        @pl.when(mine < groups - 1)
        def _():
            signal(barrier, (layer, (mine + 1) * GROUP + lax.rem(me + o, GROUP)))

    fetch_offsets = pltpu.make_async_copy(offset_ref, offset_here, local_sem.at[3])
    fetch_offsets.start()
    fetch_window = pltpu.make_async_copy(window_ref, window_here, local_sem.at[2])
    fetch_window.start()
    fetch_slab = pltpu.make_async_copy(slab_ref, slab, local_sem.at[0])
    fetch_slab.start()
    fetch_counts = pltpu.make_async_copy(density_ref, counts_ref, local_sem.at[1])
    fetch_counts.start()

    def relay(d, wanted_up, wanted_down):
        has_up = mine + d <= groups - 1
        has_down = mine - d >= 0

        @pl.when(jnp.logical_and(has_up, wanted_up))
        def _():
            pl.semaphore_wait(up_sem.at[d], 1)
            if d + 1 < groups:

                @pl.when(mine > 0)
                def _():
                    signal(up_sem.at[d + 1], (layer, me - GROUP))

        @pl.when(jnp.logical_and(has_down, wanted_down))
        def _():
            pl.semaphore_wait(down_sem.at[d], 1)
            if d + 1 < groups:

                @pl.when(mine < groups - 1)
                def _():
                    signal(down_sem.at[d + 1], (layer, me + GROUP))

    first_up = jnp.where(half == 0, half_groups - mine, 1)
    first_down = jnp.where(half == 1, mine - half_groups + 1, 1)

    def meet_near():
        @pl.when(mine == 0)
        def _():
            pl.semaphore_wait(barrier, 2 * GROUP - 1 + layers - 1)

        @pl.when(mine == groups - 1)
        def _():
            pl.semaphore_wait(barrier, 2 * GROUP - 1 + layers - 1)

        @pl.when(jnp.logical_and(mine > 0, mine < groups - 1))
        def _():
            pl.semaphore_wait(barrier, 3 * GROUP - 1 + layers - 1)
            signal(up_sem.at[2], (layer, me - GROUP))
            signal(down_sem.at[2], (layer, me + GROUP))

        for d in range(2, groups):
            relay(d, d <= first_up, d <= first_down)

    def meet_far():
        for d in range(2, groups):
            relay(d, d > first_up, d > first_down)
        for o in range(1, layers):
            signal(layer_sem, (lax.rem(layer + o, layers), me))


    lane = lax.broadcasted_iota(jnp.int32, (ROWS, CONTRIB), 1) * STEP
    row = lax.broadcasted_iota(jnp.int32, (ROWS, CONTRIB), 0)
    base_c, base_s = sincos(remainder(lane * me, facets) * width + remainder(lane * row, image), image)
    small = lax.broadcasted_iota(jnp.int32, (8, CONTRIB), 1) * STEP
    for k in range(width // ROWS):
        rot_c, rot_s = sincos(remainder(small * (ROWS * k), image), image)
        rot_c = rot_c[0:1]
        rot_s = rot_s[0:1]
        table[k * ROWS:(k + 1) * ROWS, 0:CONTRIB] = (base_c * rot_c - base_s * rot_s).astype(jnp.bfloat16)
        table[k * ROWS:(k + 1) * ROWS, CONTRIB:2 * CONTRIB] = (
            base_c * rot_s + base_s * rot_c
        ).astype(jnp.bfloat16)

    fetch_offsets.wait()
    square = (GROUP * groups, GROUP * groups)
    on_diagonal = lax.broadcasted_iota(jnp.int32, square, 0) == lax.broadcasted_iota(jnp.int32, square, 1)
    offs = jnp.sum(
        jnp.where(on_diagonal, offset_here[...].astype(jnp.float32), 0.0), axis=1, keepdims=True
    ).astype(jnp.int32)
    start = remainder(offs * me, facets) * width
    cell = lax.broadcasted_iota(jnp.int32, (facets, width), 1)
    turns = start + remainder(offs * cell, image)
    cos_a, sin_a = sincos(turns, image)
    ca[...] = cos_a
    sa[...] = sin_a

    fetch_window.wait()
    fetch_slab.wait()
    window = window_here[...]
    for p in range(2):
        wind[p * cols:(p + 1) * cols, :] = (
            (slab[0, p].astype(jnp.float32) * window).astype(jnp.bfloat16).astype(jnp.float32)
        )

    scale1 = width ** -0.5

    def encode(step, carry):
        g = outward(step)
        for k in range(width // CHUNK):
            xs = slice(k * CHUNK, (k + 1) * CHUNK)
            for t in range(GROUP):
                s = g * GROUP + t
                c_row = ca[pl.ds(s, 1), xs]
                s_row = sa[pl.ds(s, 1), xs]
                wr = wind[0:cols, xs]
                wi = wind[cols:2 * cols, xs]
                lo = t * 2 * cols
                modulated[k % 2, lo:lo + cols, :] = (wr * c_row + wi * s_row).astype(jnp.bfloat16)
                modulated[k % 2, lo + cols:lo + 2 * cols, :] = (wi * c_row - wr * s_row).astype(jnp.bfloat16)
            prod = jnp.dot(modulated[k % 2], table[xs, :], preferred_element_type=jnp.float32)
            if k == 0:
                acc[...] = prod
            else:
                acc[...] += prod
        for t in range(GROUP):
            lo = t * 2 * cols
            pr = acc[lo:lo + cols, :]
            pi = acc[lo + cols:lo + 2 * cols, :]
            real = pr[:, :CONTRIB] + pi[:, CONTRIB:]
            imag = pi[:, :CONTRIB] - pr[:, CONTRIB:]
            send1[g * GROUP + t, 0:cols, :] = (real * scale1).astype(jnp.bfloat16)
            send1[g * GROUP + t, cols:2 * cols, :] = (imag * scale1).astype(jnp.bfloat16)

        @pl.when(step == 0)
        def _():
            meet_near()

        @pl.when(step == 1)
        def _():
            meet_far()

        for t in range(GROUP):
            s = g * GROUP + t

            @pl.when(s != me)
            def _():
                pltpu.make_async_remote_copy(
                    src_ref=send1.at[s], dst_ref=recv1.at[me],
                    send_sem=ssem1.at[s], recv_sem=rsem1.at[me],
                    device_id=(layer, s), device_id_type=MESH,
                ).start()

            @pl.when(s == me)
            def _():
                recv1[s] = send1[s]

        return carry

    lax.fori_loop(0, groups, encode, 0)

    spacing = lax.broadcasted_iota(jnp.int32, (CONTRIB, SUB), 1) - STEP * lax.broadcasted_iota(
        jnp.int32, (CONTRIB, SUB), 0
    )
    scaled = spacing.astype(jnp.float32) * (1.0 / STEP)
    weight_k = 1.0 / (1.0 + scaled * scaled)
    c0, s0 = sincos(spacing, 2 * facets)
    kr[...] = c0 * weight_k
    ki[...] = s0 * weight_k
    c1, s1 = sincos(spacing, facets)
    rr[...] = c1
    ri[...] = s1

    def make_embed(f, carry):
        r = kr[...]
        i = ki[...]
        lo = pl.multiple_of(f * CONTRIB, CONTRIB)
        embed[pl.ds(lo, CONTRIB), 0:SUB] = r.astype(jnp.bfloat16)
        embed[pl.ds(lo, CONTRIB), SUB:2 * SUB] = (-i).astype(jnp.bfloat16)
        a = rr[...]
        b = ri[...]
        kr[...] = r * a - i * b
        ki[...] = r * b + i * a
        return carry

    lax.fori_loop(0, facets, make_embed, 0)
    raw[...] = jnp.zeros_like(raw)

    def gather(step, carry):
        g = inward(step)
        for t in range(GROUP):
            f = g * GROUP + t

            @pl.when(f != me)
            def _():
                pltpu.make_async_remote_copy(
                    src_ref=send1.at[f], dst_ref=recv1.at[f],
                    send_sem=ssem1.at[f], recv_sem=rsem1.at[f],
                    device_id=(layer, f), device_id_type=MESH,
                ).wait()

        lhs = jnp.concatenate([recv1[g * GROUP + t] for t in range(GROUP)], axis=1)
        lo = pl.multiple_of(g * GROUP * CONTRIB, GROUP * CONTRIB)
        raw[...] += jnp.dot(
            lhs, embed[pl.ds(lo, GROUP * CONTRIB), :], preferred_element_type=jnp.float32
        )
        return carry

    lax.fori_loop(0, groups, gather, 0)

    fetch_counts.wait()
    counts = counts_ref[0]
    weights = jnp.where(
        counts > 0, 1.0 / jnp.maximum(counts, 1).astype(jnp.float32), 0.0
    )
    sub_scale = (2 * facets) ** -0.5
    raw_r = raw[0:cols, 0:SUB] - raw[cols:2 * cols, SUB:2 * SUB]
    raw_i = raw[0:cols, SUB:2 * SUB] + raw[cols:2 * cols, 0:SUB]
    gridded = jnp.concatenate(
        [
            (raw_r * weights * sub_scale).astype(jnp.bfloat16),
            (raw_i * weights * sub_scale).astype(jnp.bfloat16),
        ],
        axis=0,
    )
    dims = (((1,), (1,)), ((), ()))

    pl.semaphore_wait(layer_sem, layers - 1)

    def scatter(step, carry):
        g = outward(step)
        lo = pl.multiple_of(g * GROUP * CONTRIB, GROUP * CONTRIB)
        er = embed[pl.ds(lo, GROUP * CONTRIB), 0:SUB]
        ei = embed[pl.ds(lo, GROUP * CONTRIB), SUB:2 * SUB]
        pr = lax.dot_general(gridded, er, dims, preferred_element_type=jnp.float32)
        pi = lax.dot_general(gridded, ei, dims, preferred_element_type=jnp.float32)
        real = ((pr[0:cols] + pi[cols:2 * cols]) * 0.5).astype(jnp.bfloat16)
        imag = ((pr[cols:2 * cols] - pi[0:cols]) * 0.5).astype(jnp.bfloat16)
        for t in range(GROUP):
            f = g * GROUP + t
            js = slice(t * CONTRIB, (t + 1) * CONTRIB)
            for l in range(layers):
                send2[f, l, 0] = real[l * part:(l + 1) * part, js]
                send2[f, l, 1] = imag[l * part:(l + 1) * part, js]
        for t in range(GROUP):
            f = g * GROUP + t
            for l in range(layers):
                own = jnp.logical_and(f == me, layer == l)

                @pl.when(jnp.logical_not(own))
                def _():
                    pltpu.make_async_remote_copy(
                        src_ref=send2.at[f, l], dst_ref=recv2.at[layer, me],
                        send_sem=ssem2.at[l, f], recv_sem=rsem2.at[layer, me],
                        device_id=(l, f), device_id_type=MESH,
                    ).start()

                @pl.when(own)
                def _():
                    recv2[layer, me] = send2[f, l]

        return carry

    lax.fori_loop(0, groups, scatter, 0)

    out_ref[...] = jnp.zeros_like(out_ref)
    out_scale = (facets * CONTRIB) ** -0.5

    def adjoint(step, carry):
        g = inward(step)
        tops = []
        for t in range(GROUP):
            s = g * GROUP + t
            for l in range(layers):
                own = jnp.logical_and(s == me, layer == l)

                @pl.when(jnp.logical_not(own))
                def _():
                    pltpu.make_async_remote_copy(
                        src_ref=send2.at[s, l], dst_ref=recv2.at[l, s],
                        send_sem=ssem2.at[l, s], recv_sem=rsem2.at[l, s],
                        device_id=(l, s), device_id_type=MESH,
                    ).wait()

        for t in range(GROUP):
            s = g * GROUP + t
            br = recv2[0, s, 0].astype(jnp.float32)
            bi = recv2[0, s, 1].astype(jnp.float32)
            for l in range(1, layers):
                br = br + recv2[l, s, 0].astype(jnp.float32)
                bi = bi + recv2[l, s, 1].astype(jnp.float32)
            tops.append(jnp.concatenate([br, -bi], axis=1))
            tops.append(jnp.concatenate([bi, br], axis=1))
        lhs = jnp.concatenate(tops, axis=0).astype(jnp.bfloat16)
        for k in range(width // CHUNK):
            xs = slice(k * CHUNK, (k + 1) * CHUNK)
            prod = lax.dot_general(lhs, table[xs, :], dims, preferred_element_type=jnp.float32)
            out_r = out_ref[0, :, xs]
            out_i = out_ref[1, :, xs]
            for t in range(GROUP):
                s = g * GROUP + t
                c_row = ca[pl.ds(s, 1), xs]
                s_row = sa[pl.ds(s, 1), xs]
                gr = prod[(2 * t) * part:(2 * t + 1) * part]
                gi = prod[(2 * t + 1) * part:(2 * t + 2) * part]
                out_r = out_r + (c_row * gr - s_row * gi)
                out_i = out_i + (c_row * gi + s_row * gr)
            factor = jnp.where(step == groups - 1, window_here[:, xs] * out_scale, 1.0)
            out_ref[0, :, xs] = out_r * factor
            out_ref[1, :, xs] = out_i * factor
        return carry

    lax.fori_loop(0, groups, adjoint, 0)


def shards(slabs, window, density, offsets):
    facets = lax.axis_size("facet")
    layers = lax.axis_size("layer")
    cols = slabs.shape[2]
    width = slabs.shape[3]
    part = cols // layers
    f32, bf16 = jnp.float32, jnp.bfloat16
    summed = pl.pallas_call(
        functools.partial(kernel, layers, facets, cols, width),
        out_shape=jax.ShapeDtypeStruct((2, part, width), f32),
        in_specs=[pl.BlockSpec(memory_space=pltpu.HBM)] * 4,
        out_specs=pl.BlockSpec(memory_space=pltpu.VMEM),
        scratch_shapes=[
            pltpu.VMEM(slabs.shape, bf16),
            pltpu.VMEM(density.shape, jnp.int32),
            pltpu.VMEM((1, width), f32),
            pltpu.VMEM((1, facets), jnp.int32),
            pltpu.VMEM((2 * cols, width), f32),
            pltpu.VMEM((facets, width), f32),
            pltpu.VMEM((facets, width), f32),
            pltpu.VMEM((width, 2 * CONTRIB), bf16),
            pltpu.VMEM((2, GROUP * 2 * cols, CHUNK), bf16),
            pltpu.VMEM((GROUP * 2 * cols, 2 * CONTRIB), f32),
            pltpu.VMEM((facets, 2 * cols, CONTRIB), bf16),
            pltpu.VMEM((facets, 2 * cols, CONTRIB), bf16),
            pltpu.VMEM((facets * CONTRIB, 2 * SUB), bf16),
            pltpu.VMEM((CONTRIB, SUB), f32),
            pltpu.VMEM((CONTRIB, SUB), f32),
            pltpu.VMEM((CONTRIB, SUB), f32),
            pltpu.VMEM((CONTRIB, SUB), f32),
            pltpu.VMEM((2 * cols, 2 * SUB), f32),
            pltpu.VMEM((facets, layers, 2, part, CONTRIB), bf16),
            pltpu.VMEM((layers, facets, 2, part, CONTRIB), bf16),
            pltpu.SemaphoreType.DMA((facets,)),
            pltpu.SemaphoreType.DMA((facets,)),
            pltpu.SemaphoreType.DMA((layers, facets)),
            pltpu.SemaphoreType.DMA((layers, facets)),
            pltpu.SemaphoreType.DMA((4,)),
            pltpu.SemaphoreType.REGULAR((facets // GROUP,)),
            pltpu.SemaphoreType.REGULAR((facets // GROUP,)),
            pltpu.SemaphoreType.REGULAR,
        ],
        compiler_params=pltpu.CompilerParams(
            collective_id=0, has_side_effects=True, vmem_limit_bytes=(14 + facets) * 1024 * 1024
        ),
    )(
        *(
            pltpu.with_memory_space_constraint(x, pltpu.HBM)
            for x in (slabs, window[None, :], density, offsets[None, :])
        )
    )
    return summed


def solution(mesh):
    placed = (P("layer", None, None, "facet"), P("facet"), P("layer", None, "facet"), P())
    return jax.shard_map(
        shards, mesh=mesh, in_specs=placed, out_specs=P(None, "layer", "facet"), check_vma=False
    )
```

```python
import functools
import math

import jax
import jax.numpy as jnp
from jax import lax
from jax.experimental import pallas as pl
from jax.experimental.pallas import tpu as pltpu
from jax.sharding import PartitionSpec as P

CONTRIB = 128
SUB = 512
GROUP = 4
PIECE = 2
PIECES = GROUP // PIECE
CHUNK = 512
ROWS = 256
STEP = SUB // CONTRIB

MESH = pl.DeviceIdType.MESH


def sincos(turns, period):
    quarter = jnp.floor(turns.astype(jnp.float32) * (4.0 / period) + 0.5).astype(jnp.int32)
    rest = 4 * turns - quarter * period
    y = rest.astype(jnp.float32) * (0.5 * math.pi / period)
    z = y * y
    s = y + y * z * (-1.0 / 6 + z * (1.0 / 120 + z * (-1.0 / 5040 + z * (1.0 / 362880))))
    c = 1.0 + z * (-0.5 + z * (1.0 / 24 + z * (-1.0 / 720 + z * (1.0 / 40320))))
    odd = (quarter & 1) == 1
    cos_abs = jnp.where(odd, s, c)
    sin_abs = jnp.where(odd, c, s)
    cos_part = jnp.where(((quarter + 1) & 2) == 2, -cos_abs, cos_abs)
    sin_part = jnp.where((quarter & 2) == 2, -sin_abs, sin_abs)
    return cos_part, sin_part


def remainder(value, period):
    return value - jnp.floor(value.astype(jnp.float32) * (1.0 / period)).astype(jnp.int32) * period


def kernel(
    layers, facets, cols, width,
    slab_ref, window_ref, density_ref, offset_ref,
    out_ref,
    slab, counts_ref, window_here, offset_here, wind, ca, sa, table, modulated, acc,
    send1, recv1, embed, kr, ki, rr, ri, raw,
    send2, recv2,
    ssem1, rsem1, ssem2, rsem2, local_sem, up_sem, down_sem, layer_sem,
):
    layer = lax.axis_index("layer")
    me = lax.axis_index("facet")
    image = facets * width
    groups = facets // GROUP
    part = cols // layers
    mine = me // GROUP
    half = mine // (groups // 2)
    half_groups = groups // 2

    def outward(step):
        return jnp.where(
            half == 0,
            lax.rem(half_groups + step, groups),
            lax.rem(half_groups - 1 - step + groups, groups),
        )

    def inward(step):
        return jnp.where(half == 0, step, groups - 1 - step)

    def signal(sem, where):
        pl.semaphore_signal(sem, inc=1, device_id=where, device_id_type=MESH)

    barrier = pltpu.get_barrier_semaphore()
    for o in range(1, layers):
        signal(barrier, (lax.rem(layer + o, layers), me))
    for o in range(1, GROUP):
        signal(barrier, (layer, mine * GROUP + lax.rem(me + o, GROUP)))
    for o in range(GROUP):

        @pl.when(mine > 0)
        def _():
            signal(barrier, (layer, (mine - 1) * GROUP + lax.rem(me + o, GROUP)))

        @pl.when(mine < groups - 1)
        def _():
            signal(barrier, (layer, (mine + 1) * GROUP + lax.rem(me + o, GROUP)))

    fetch_offsets = pltpu.make_async_copy(offset_ref, offset_here, local_sem.at[3])
    fetch_offsets.start()
    fetch_window = pltpu.make_async_copy(window_ref, window_here, local_sem.at[2])
    fetch_window.start()
    fetch_slab = pltpu.make_async_copy(slab_ref, slab, local_sem.at[0])
    fetch_slab.start()
    fetch_counts = pltpu.make_async_copy(density_ref, counts_ref, local_sem.at[1])
    fetch_counts.start()

    def relay(d, wanted_up, wanted_down):
        has_up = mine + d <= groups - 1
        has_down = mine - d >= 0

        @pl.when(jnp.logical_and(has_up, wanted_up))
        def _():
            pl.semaphore_wait(up_sem.at[d], 1)
            if d + 1 < groups:

                @pl.when(mine > 0)
                def _():
                    signal(up_sem.at[d + 1], (layer, me - GROUP))

        @pl.when(jnp.logical_and(has_down, wanted_down))
        def _():
            pl.semaphore_wait(down_sem.at[d], 1)
            if d + 1 < groups:

                @pl.when(mine < groups - 1)
                def _():
                    signal(down_sem.at[d + 1], (layer, me + GROUP))

    first_up = jnp.where(half == 0, half_groups - mine, 1)
    first_down = jnp.where(half == 1, mine - half_groups + 1, 1)

    def meet_near():
        @pl.when(mine == 0)
        def _():
            pl.semaphore_wait(barrier, 2 * GROUP - 1 + layers - 1)

        @pl.when(mine == groups - 1)
        def _():
            pl.semaphore_wait(barrier, 2 * GROUP - 1 + layers - 1)

        @pl.when(jnp.logical_and(mine > 0, mine < groups - 1))
        def _():
            pl.semaphore_wait(barrier, 3 * GROUP - 1 + layers - 1)
            signal(up_sem.at[2], (layer, me - GROUP))
            signal(down_sem.at[2], (layer, me + GROUP))

        for d in range(2, groups):
            relay(d, d <= first_up, d <= first_down)

    def meet_far():
        for d in range(2, groups):
            relay(d, d > first_up, d > first_down)
        for o in range(1, layers):
            signal(layer_sem, (lax.rem(layer + o, layers), me))


    lane = lax.broadcasted_iota(jnp.int32, (ROWS, CONTRIB), 1) * STEP
    row = lax.broadcasted_iota(jnp.int32, (ROWS, CONTRIB), 0)
    base_c, base_s = sincos(remainder(lane * me, facets) * width + remainder(lane * row, image), image)
    small = lax.broadcasted_iota(jnp.int32, (8, CONTRIB), 1) * STEP
    for k in range(width // ROWS):
        rot_c, rot_s = sincos(remainder(small * (ROWS * k), image), image)
        rot_c = rot_c[0:1]
        rot_s = rot_s[0:1]
        table[k * ROWS:(k + 1) * ROWS, 0:CONTRIB] = (base_c * rot_c - base_s * rot_s).astype(jnp.bfloat16)
        table[k * ROWS:(k + 1) * ROWS, CONTRIB:2 * CONTRIB] = (
            base_c * rot_s + base_s * rot_c
        ).astype(jnp.bfloat16)

    fetch_offsets.wait()
    square = (GROUP * groups, GROUP * groups)
    on_diagonal = lax.broadcasted_iota(jnp.int32, square, 0) == lax.broadcasted_iota(jnp.int32, square, 1)
    offs = jnp.sum(
        jnp.where(on_diagonal, offset_here[...].astype(jnp.float32), 0.0), axis=1, keepdims=True
    ).astype(jnp.int32)
    start = remainder(offs * me, facets) * width
    cell = lax.broadcasted_iota(jnp.int32, (facets, width), 1)
    turns = start + remainder(offs * cell, image)
    cos_a, sin_a = sincos(turns, image)
    ca[...] = cos_a
    sa[...] = sin_a

    fetch_window.wait()
    fetch_slab.wait()
    window = window_here[...]
    for p in range(2):
        wind[p * cols:(p + 1) * cols, :] = (
            (slab[0, p].astype(jnp.float32) * window).astype(jnp.bfloat16).astype(jnp.float32)
        )

    scale1 = width ** -0.5

    def encode(step, carry):
        g = outward(step)
        for k in range(width // CHUNK):
            xs = slice(k * CHUNK, (k + 1) * CHUNK)
            for t in range(GROUP):
                s = g * GROUP + t
                c_row = ca[pl.ds(s, 1), xs]
                s_row = sa[pl.ds(s, 1), xs]
                wr = wind[0:cols, xs]
                wi = wind[cols:2 * cols, xs]
                lo = t * 2 * cols
                modulated[k % 2, lo:lo + cols, :] = (wr * c_row + wi * s_row).astype(jnp.bfloat16)
                modulated[k % 2, lo + cols:lo + 2 * cols, :] = (wi * c_row - wr * s_row).astype(jnp.bfloat16)
            prod = jnp.dot(modulated[k % 2], table[xs, :], preferred_element_type=jnp.float32)
            if k == 0:
                acc[...] = prod
            else:
                acc[...] += prod
        for t in range(GROUP):
            lo = t * 2 * cols
            pr = acc[lo:lo + cols, :]
            pi = acc[lo + cols:lo + 2 * cols, :]
            real = pr[:, :CONTRIB] + pi[:, CONTRIB:]
            imag = pi[:, :CONTRIB] - pr[:, CONTRIB:]
            send1[g * GROUP + t, 0:cols, :] = (real * scale1).astype(jnp.bfloat16)
            send1[g * GROUP + t, cols:2 * cols, :] = (imag * scale1).astype(jnp.bfloat16)

        @pl.when(step == 0)
        def _():
            meet_near()

        @pl.when(step == 1)
        def _():
            meet_far()

        for t in range(GROUP):
            s = g * GROUP + t

            @pl.when(s != me)
            def _():
                pltpu.make_async_remote_copy(
                    src_ref=send1.at[s], dst_ref=recv1.at[me],
                    send_sem=ssem1.at[s], recv_sem=rsem1.at[me],
                    device_id=(layer, s), device_id_type=MESH,
                ).start()

            @pl.when(s == me)
            def _():
                recv1[s] = send1[s]

        return carry

    lax.fori_loop(0, groups, encode, 0)

    spacing = lax.broadcasted_iota(jnp.int32, (CONTRIB, SUB), 1) - STEP * lax.broadcasted_iota(
        jnp.int32, (CONTRIB, SUB), 0
    )
    scaled = spacing.astype(jnp.float32) * (1.0 / STEP)
    weight_k = 1.0 / (1.0 + scaled * scaled)
    c0, s0 = sincos(spacing, 2 * facets)
    kr[...] = c0 * weight_k
    ki[...] = s0 * weight_k
    c1, s1 = sincos(spacing, facets)
    rr[...] = c1
    ri[...] = s1

    def make_embed(f, carry):
        r = kr[...]
        i = ki[...]
        lo = pl.multiple_of(f * CONTRIB, CONTRIB)
        embed[pl.ds(lo, CONTRIB), 0:SUB] = r.astype(jnp.bfloat16)
        embed[pl.ds(lo, CONTRIB), SUB:2 * SUB] = (-i).astype(jnp.bfloat16)
        a = rr[...]
        b = ri[...]
        kr[...] = r * a - i * b
        ki[...] = r * b + i * a
        return carry

    lax.fori_loop(0, facets, make_embed, 0)
    raw[...] = jnp.zeros_like(raw)

    def gather(step, carry):
        first = inward(step // PIECES) * GROUP + lax.rem(step, PIECES) * PIECE
        for t in range(PIECE):
            f = first + t

            @pl.when(f != me)
            def _():
                pltpu.make_async_remote_copy(
                    src_ref=send1.at[f], dst_ref=recv1.at[f],
                    send_sem=ssem1.at[f], recv_sem=rsem1.at[f],
                    device_id=(layer, f), device_id_type=MESH,
                ).wait()

        lhs = jnp.concatenate([recv1[first + t] for t in range(PIECE)], axis=1)
        lo = pl.multiple_of(first * CONTRIB, PIECE * CONTRIB)
        raw[...] += jnp.dot(
            lhs, embed[pl.ds(lo, PIECE * CONTRIB), :], preferred_element_type=jnp.float32
        )
        return carry

    lax.fori_loop(0, groups * PIECES, gather, 0)

    fetch_counts.wait()
    counts = counts_ref[0]
    weights = jnp.where(
        counts > 0, 1.0 / jnp.maximum(counts, 1).astype(jnp.float32), 0.0
    )
    sub_scale = (2 * facets) ** -0.5
    raw_r = raw[0:cols, 0:SUB] - raw[cols:2 * cols, SUB:2 * SUB]
    raw_i = raw[0:cols, SUB:2 * SUB] + raw[cols:2 * cols, 0:SUB]
    gridded = jnp.concatenate(
        [
            (raw_r * weights * sub_scale).astype(jnp.bfloat16),
            (raw_i * weights * sub_scale).astype(jnp.bfloat16),
        ],
        axis=0,
    )
    dims = (((1,), (1,)), ((), ()))

    pl.semaphore_wait(layer_sem, layers - 1)

    def scatter(step, carry):
        first = outward(step // PIECES) * GROUP + lax.rem(step, PIECES) * PIECE
        lo = pl.multiple_of(first * CONTRIB, PIECE * CONTRIB)
        er = embed[pl.ds(lo, PIECE * CONTRIB), 0:SUB]
        ei = embed[pl.ds(lo, PIECE * CONTRIB), SUB:2 * SUB]
        pr = lax.dot_general(gridded, er, dims, preferred_element_type=jnp.float32)
        pi = lax.dot_general(gridded, ei, dims, preferred_element_type=jnp.float32)
        real = ((pr[0:cols] + pi[cols:2 * cols]) * 0.5).astype(jnp.bfloat16)
        imag = ((pr[cols:2 * cols] - pi[0:cols]) * 0.5).astype(jnp.bfloat16)
        for t in range(PIECE):
            f = first + t
            js = slice(t * CONTRIB, (t + 1) * CONTRIB)
            for l in range(layers):
                send2[f, l, 0] = real[l * part:(l + 1) * part, js]
                send2[f, l, 1] = imag[l * part:(l + 1) * part, js]
        for t in range(PIECE):
            f = first + t
            for l in range(layers):
                own = jnp.logical_and(f == me, layer == l)

                @pl.when(jnp.logical_not(own))
                def _():
                    pltpu.make_async_remote_copy(
                        src_ref=send2.at[f, l], dst_ref=recv2.at[layer, me],
                        send_sem=ssem2.at[l, f], recv_sem=rsem2.at[layer, me],
                        device_id=(l, f), device_id_type=MESH,
                    ).start()

                @pl.when(own)
                def _():
                    recv2[layer, me] = send2[f, l]

        return carry

    lax.fori_loop(0, groups * PIECES, scatter, 0)

    out_ref[...] = jnp.zeros_like(out_ref)
    out_scale = (facets * CONTRIB) ** -0.5

    def adjoint(step, carry):
        g = inward(step)
        tops = []
        for t in range(GROUP):
            s = g * GROUP + t
            for l in range(layers):
                own = jnp.logical_and(s == me, layer == l)

                @pl.when(jnp.logical_not(own))
                def _():
                    pltpu.make_async_remote_copy(
                        src_ref=send2.at[s, l], dst_ref=recv2.at[l, s],
                        send_sem=ssem2.at[l, s], recv_sem=rsem2.at[l, s],
                        device_id=(l, s), device_id_type=MESH,
                    ).wait()

        for t in range(GROUP):
            s = g * GROUP + t
            br = recv2[0, s, 0].astype(jnp.float32)
            bi = recv2[0, s, 1].astype(jnp.float32)
            for l in range(1, layers):
                br = br + recv2[l, s, 0].astype(jnp.float32)
                bi = bi + recv2[l, s, 1].astype(jnp.float32)
            tops.append(jnp.concatenate([br, -bi], axis=1))
            tops.append(jnp.concatenate([bi, br], axis=1))
        lhs = jnp.concatenate(tops, axis=0).astype(jnp.bfloat16)
        for k in range(width // CHUNK):
            xs = slice(k * CHUNK, (k + 1) * CHUNK)
            prod = lax.dot_general(lhs, table[xs, :], dims, preferred_element_type=jnp.float32)
            out_r = out_ref[0, :, xs]
            out_i = out_ref[1, :, xs]
            for t in range(GROUP):
                s = g * GROUP + t
                c_row = ca[pl.ds(s, 1), xs]
                s_row = sa[pl.ds(s, 1), xs]
                gr = prod[(2 * t) * part:(2 * t + 1) * part]
                gi = prod[(2 * t + 1) * part:(2 * t + 2) * part]
                out_r = out_r + (c_row * gr - s_row * gi)
                out_i = out_i + (c_row * gi + s_row * gr)
            factor = jnp.where(step == groups - 1, window_here[:, xs] * out_scale, 1.0)
            out_ref[0, :, xs] = out_r * factor
            out_ref[1, :, xs] = out_i * factor
        return carry

    lax.fori_loop(0, groups, adjoint, 0)


def shards(slabs, window, density, offsets):
    facets = lax.axis_size("facet")
    layers = lax.axis_size("layer")
    cols = slabs.shape[2]
    width = slabs.shape[3]
    part = cols // layers
    f32, bf16 = jnp.float32, jnp.bfloat16
    summed = pl.pallas_call(
        functools.partial(kernel, layers, facets, cols, width),
        out_shape=jax.ShapeDtypeStruct((2, part, width), f32),
        in_specs=[pl.BlockSpec(memory_space=pltpu.HBM)] * 4,
        out_specs=pl.BlockSpec(memory_space=pltpu.VMEM),
        scratch_shapes=[
            pltpu.VMEM(slabs.shape, bf16),
            pltpu.VMEM(density.shape, jnp.int32),
            pltpu.VMEM((1, width), f32),
            pltpu.VMEM((1, facets), jnp.int32),
            pltpu.VMEM((2 * cols, width), f32),
            pltpu.VMEM((facets, width), f32),
            pltpu.VMEM((facets, width), f32),
            pltpu.VMEM((width, 2 * CONTRIB), bf16),
            pltpu.VMEM((2, GROUP * 2 * cols, CHUNK), bf16),
            pltpu.VMEM((GROUP * 2 * cols, 2 * CONTRIB), f32),
            pltpu.VMEM((facets, 2 * cols, CONTRIB), bf16),
            pltpu.VMEM((facets, 2 * cols, CONTRIB), bf16),
            pltpu.VMEM((facets * CONTRIB, 2 * SUB), bf16),
            pltpu.VMEM((CONTRIB, SUB), f32),
            pltpu.VMEM((CONTRIB, SUB), f32),
            pltpu.VMEM((CONTRIB, SUB), f32),
            pltpu.VMEM((CONTRIB, SUB), f32),
            pltpu.VMEM((2 * cols, 2 * SUB), f32),
            pltpu.VMEM((facets, layers, 2, part, CONTRIB), bf16),
            pltpu.VMEM((layers, facets, 2, part, CONTRIB), bf16),
            pltpu.SemaphoreType.DMA((facets,)),
            pltpu.SemaphoreType.DMA((facets,)),
            pltpu.SemaphoreType.DMA((layers, facets)),
            pltpu.SemaphoreType.DMA((layers, facets)),
            pltpu.SemaphoreType.DMA((4,)),
            pltpu.SemaphoreType.REGULAR((facets // GROUP,)),
            pltpu.SemaphoreType.REGULAR((facets // GROUP,)),
            pltpu.SemaphoreType.REGULAR,
        ],
        compiler_params=pltpu.CompilerParams(
            collective_id=0, has_side_effects=True, vmem_limit_bytes=(14 + facets) * 1024 * 1024
        ),
    )(
        *(
            pltpu.with_memory_space_constraint(x, pltpu.HBM)
            for x in (slabs, window[None, :], density, offsets[None, :])
        )
    )
    return summed


def solution(mesh):
    placed = (P("layer", None, None, "facet"), P("facet"), P("layer", None, "facet"), P())
    return jax.shard_map(
        shards, mesh=mesh, in_specs=placed, out_specs=P(None, "layer", "facet"), check_vma=False
    )
```
